32 devices in a mesh: in: 8 (over z, y), out: 4 (over x, core).
Axes of the slice: x: 2, y: 2, z: 4, core: 2. Of those that a mesh axis runs over, the one named last changes fastest.
Arguments:
- inputs: bfloat16 [64, 12288], P('out', 'in'), may hold values from -6 to 6
- weight: float32 [12288, 36864], P('in', 'out'), may hold values from -6 to 6
- out_grad: bfloat16 [64, 36864], P('in', 'out'), may hold values from -6 to 6
- step_size: float32 [], replicated, may hold values from 1 to 8
Outputs:
- projected: bfloat16 [64, 36864], P('in', 'out')
- input_grad: bfloat16 [64, 12288], P('out', 'in')
- new_weight: float32 [12288, 36864], P('in', 'out')
The draws below stay inside these ranges and needn't reach their ends.
All inputs are finite; a program needn't handle non-finite values.
Results may differ from the reference program's by a relative error of at most 0.023.
Values may be sent and summed in bfloat16 or wider, within the bound.
A program may use at most 192 MiB of HBM per device.

```python
import math
import jax
import jax.numpy as jnp
from jax import lax

D = 12288
F = 36864
ROWS = 64
N_IN = 8
N_OUT = 4


def shard_levels(rng, extent, pieces, low, largest):
    def one(position, blocks):
        steps = jax.random.uniform(jax.random.fold_in(jax.random.fold_in(rng, 6), position), (blocks,), jnp.float32, low / len(pieces), largest / len(pieces))
        return jnp.repeat(jnp.exp(steps), extent[position] // blocks).reshape((-1,) + (1,) * (len(extent) - position - 1))

    gain = one(*pieces[0])
    for cut in pieces[1:]:
        gain = gain * one(*cut)
    return gain


def centred(rng, extent, width, bound, split=(), kind=jnp.bfloat16):
    gain = shard_levels(rng, extent, split, -0.22, 0.18) if split else 1.0
    values = jax.random.normal(rng, extent, jnp.float32) * width * gain
    return jnp.minimum(jnp.maximum(values, -bound), bound).astype(kind)


def setup_inputs(seed: int = 0) -> dict:
    key_list = jax.random.split(jax.random.key(seed), 5)
    inputs = centred(key_list[0], (ROWS, D), 1.0, 6.0, ((0, 4), (1, 8)))
    weight = centred(key_list[1], (D, F), 1.0, 6.0, ((0, 8), (1, 4)), jnp.float32)
    out_grad = centred(key_list[2], (ROWS, F), 1.0, 6.0, ((0, 8), (1, 4)))
    step_size = jnp.clip(jnp.exp(jax.random.uniform(key_list[3], (), jnp.float32, math.log(1.0), math.log(8.0))), 1.0, 8.0)
    return {"inputs": inputs, "weight": weight, "out_grad": out_grad, "step_size": step_size}


def reference(inputs, weight, out_grad, step_size):
    scale = float(D) ** -0.5
    low_weight = weight.astype(jnp.bfloat16)
    width_block = D // N_IN
    feature_block = F // N_OUT

    def forward_add(total, index):
        start = (index * width_block).astype(jnp.int32)
        left = lax.dynamic_slice_in_dim(inputs, start, width_block, 1)
        right = lax.dynamic_slice_in_dim(low_weight, start, width_block, 0)
        piece = (jnp.dot(left, right, preferred_element_type=jnp.float32) * scale).astype(jnp.bfloat16)
        return total + piece.astype(jnp.float32), None

    summed, unused = lax.scan(forward_add, jnp.zeros((ROWS, F), jnp.float32), jnp.arange(N_IN, dtype=jnp.int32))
    projected = summed.astype(jnp.bfloat16)

    def backward_add(total, index):
        start = (index * feature_block).astype(jnp.int32)
        left = lax.dynamic_slice_in_dim(out_grad, start, feature_block, 1)
        right = lax.dynamic_slice_in_dim(low_weight, start, feature_block, 1)
        back = lax.dot_general(left, right, (((1,), (1,)), ((), ())), preferred_element_type=jnp.float32)
        piece = (back * scale).astype(jnp.bfloat16)
        return total + piece.astype(jnp.float32), None

    back_sum, unused2 = lax.scan(backward_add, jnp.zeros((ROWS, D), jnp.float32), jnp.arange(N_OUT, dtype=jnp.int32))
    input_grad = back_sum.astype(jnp.bfloat16)
    weight_grad = lax.dot_general(inputs, out_grad, (((0,), (0,)), ((), ())), preferred_element_type=jnp.float32) * scale
    new_weight = weight - step_size * weight_grad
    return projected, input_grad, new_weight
```

```python
import functools

import jax
import jax.numpy as jnp
from jax import lax
from jax.experimental import pallas as pl
from jax.experimental.pallas import tpu as pltpu
from jax.sharding import PartitionSpec as P

MESH = pl.DeviceIdType.MESH
BF16, F32 = jnp.bfloat16, jnp.float32
LEFT, RIGHT, ACROSS = 0, 1, 2


def fit(extent, unit, most):
    return max(c for c in range(unit, most + 1, unit) if extent % c == 0)


def read_side(
    n_in, n_out, scale, first,
    step_ref, x_ref, g_ref, w_ref,
    wv_ref, factor_ref, xt_ref, gall_ref, *rest,
):
    line = n_in // 2
    ysum = rest[:line]
    ipart = rest[line : line + n_out]
    (x3, x64, g3, part, send, recv, kept, back,
     w_sem, xs_sem, xr_sem, gs_sem, gr_sem, ys_sem, yr_sem) = rest[line + n_out :]
    depth, width = wv_ref.shape
    rows = g_ref.shape[0]
    rows_x = x_ref.shape[0]
    strips, _, strip = send.shape
    sub = fit(strip, 128, 512)
    me = lax.axis_index("in")
    mo = lax.axis_index("out")
    p, y = me // 2, me % 2
    pair = me + 1 - 2 * y

    def w_copy(s):
        cols = pl.ds(s * strip, strip)
        return pltpu.make_async_copy(w_ref.at[:, cols], wv_ref.at[:, cols], w_sem.at[s])

    for s in range(strips):
        w_copy(s).start()

    barrier = pltpu.get_barrier_semaphore()
    peers = [{"in": pair}, {"in": lax.rem(me + 2, n_in)}, {"in": lax.rem(me + n_in - 2, n_in)}]
    peers += [{"out": lax.rem(mo + t, n_out)} for t in range(1, n_out)]
    for peer in peers:
        pl.semaphore_signal(barrier, inc=1, device_id=peer, device_id_type=MESH)
    pl.semaphore_wait(barrier, len(peers))

    def x_copy(t):
        return pltpu.make_async_remote_copy(
            src_ref=x_ref, dst_ref=x3.at[mo], send_sem=xs_sem.at[t], recv_sem=xr_sem.at[mo],
            device_id={"out": lax.rem(mo + t, n_out)}, device_id_type=MESH)

    def x_arrival(t):
        o = lax.rem(mo + n_out - t, n_out)
        return pltpu.make_async_remote_copy(
            src_ref=x_ref, dst_ref=x3.at[o], send_sem=xs_sem.at[t], recv_sem=xr_sem.at[o],
            device_id={"out": o}, device_id_type=MESH)

    for t in range(1, n_out):
        x_copy(t).start()

    groups = [pl.ds(0, first), pl.ds(first, width - first)]

    def g_copy(i, group, way, own=False):
        cols = groups[group]
        target = {LEFT: lax.rem(me + n_in - 2, n_in), RIGHT: lax.rem(me + 2, n_in), ACROSS: pair}[way]
        here = g3.at[i, :, cols]
        return pltpu.make_async_remote_copy(
            src_ref=g_ref.at[:, cols] if own else here, dst_ref=here,
            send_sem=gs_sem.at[i, group, way], recv_sem=gr_sem.at[i, group],
            device_id={"in": target}, device_id_type=MESH)

    def outward(i, group, way, verb, own=False):
        edge = (p < line - 1) if way == RIGHT else (p > 0)

        @pl.when(edge)
        def _():
            getattr(g_copy(i, group, way, own), verb)()

    def origin_step(verb):
        for group in (1, 0):
            getattr(g_copy(me, group, ACROSS, True), verb)()
        for group in (1, 0):
            outward(me, group, LEFT, verb, True)
            outward(me, group, RIGHT, verb, True)

    def pair_step(verb):
        if verb == "start":
            g_copy(pair, 1, ACROSS).wait_recv()
        outward(pair, 1, LEFT, verb)
        outward(pair, 1, RIGHT, verb)

    def hop_step(s, verb):
        for way in (RIGHT, LEFT):
            o = p - s if way == RIGHT else p + s

            @pl.when((o >= 0) & (o < line))
            def _():
                for par in (y, 1 - y):
                    i = o * 2 + par
                    if verb == "start":
                        g_copy(i, 1, way).wait_recv()
                    outward(i, 1, way, verb)
                i = o * 2 + y
                if verb == "start":
                    g_copy(i, 0, way).wait_recv()
                outward(i, 0, way, verb)
                getattr(g_copy(i, 0, ACROSS), verb)()

    origin_step("start")
    factor_ref[...] = jnp.full(factor_ref.shape, step_ref[0] * scale, F32)
    x3[mo] = x_ref[...]
    g3[me] = g_ref[...]

    for t in range(1, n_out):
        x_arrival(t).wait_recv()
    rows_all = jnp.concatenate([x3[o].astype(F32) for o in range(n_out)], axis=0)
    x64[...] = rows_all.astype(BF16)
    xt_ref[...] = jnp.transpose(rows_all).astype(BF16)

    def y_copy(s):
        return pltpu.make_async_remote_copy(
            src_ref=send.at[s], dst_ref=recv.at[s], send_sem=ys_sem.at[s], recv_sem=yr_sem.at[s],
            device_id={"in": pair}, device_id_type=MESH)

    def forward(s):
        w_copy(s).wait()

        @pl.loop(0, strip // sub)
        def _(b):
            c = pl.multiple_of(b * sub, sub)
            low = wv_ref[:, pl.ds(s * strip + c, sub)].astype(BF16)
            out = jnp.dot(x64[...], low, preferred_element_type=F32) * scale
            part[:, :, :, pl.ds(c, sub)] = out.reshape(line, 2, rows, sub)

        send[s] = part[:, 1 - y].reshape(line * rows, strip).astype(BF16)
        y_copy(s).start()
        kept[s] = part[:, y]

    def settle(s):
        y_copy(s).wait_recv()
        kept[s] = kept[s] + recv[s].astype(F32).reshape(line, rows, strip)
        for t in range(line):
            ysum[t][:, pl.ds(s * strip, strip)] = kept[s, lax.rem(p + t, line)].astype(BF16)

    steps = [lambda: pair_step("start")]
    steps += [functools.partial(hop_step, s, "start") for s in range(1, line)]
    done = 0
    for s in range(strips):
        forward(s)
        while done < len(steps) and done * max(strips - 2, 1) < (s + 1) * len(steps):
            steps[done]()
            done += 1
    while done < len(steps):
        steps[done]()
        done += 1

    @pl.loop(0, line)
    def _(o):
        g_copy(o * 2 + 1 - y, 0, ACROSS).wait_recv()

    chunk = fit(width, 128, 512)

    @pl.loop(0, width // chunk)
    def _(b):
        cols = pl.ds(pl.multiple_of(b * chunk, chunk), chunk)
        gall_ref[:, cols] = jnp.concatenate(
            [g3[i, :, cols].astype(F32) for i in range(n_in)], axis=0).astype(BF16)

    back[...] = jnp.zeros_like(back)

    @pl.loop(0, width // chunk)
    def _(b):
        cols = pl.ds(pl.multiple_of(b * chunk, chunk), chunk)
        low = wv_ref[:, cols].astype(BF16)
        out = lax.dot_general(gall_ref[:, cols], low, (((1,), (1,)), ((), ())),
                              preferred_element_type=F32)
        back[...] += out.reshape(n_out, rows_x, depth)

    for t in range(n_out):
        ipart[t][...] = (back[lax.rem(mo + t, n_out)] * scale).astype(BF16)

    for s in range(strips):
        settle(s)

    for t in range(1, n_out):
        x_copy(t).wait_send()
    origin_step("wait_send")
    pair_step("wait_send")
    for s in range(1, line):
        hop_step(s, "wait_send")
    for s in range(strips):
        y_copy(s).wait_send()


def write_side(factor_ref, w_ref, xt_ref, g_ref, o_ref, stage, sem):
    slots, high, wide = stage.shape
    depth, width = w_ref.shape
    across = width // wide
    part = fit(wide, 128, 256)
    tiles = (depth // high) * across
    factor = factor_ref[0:1, 0:1]

    def out_copy(i):
        r = pl.multiple_of((i // across) * high, high)
        c = pl.multiple_of((i % across) * wide, wide)
        return pltpu.make_async_copy(
            stage.at[i % slots], o_ref.at[pl.ds(r, high), pl.ds(c, wide)], sem.at[i % slots])

    @pl.loop(0, tiles)
    def _(i):
        @pl.when(i >= slots)
        def _():
            out_copy(i - slots).wait()

        r = pl.multiple_of((i // across) * high, high)
        c = pl.multiple_of((i % across) * wide, wide)
        left = xt_ref[pl.ds(r, high), :]
        for k in range(0, wide, part):
            cols = pl.ds(c + k, part)
            grad = jnp.dot(left, g_ref[:, cols], preferred_element_type=F32)
            stage[i % slots, :, pl.ds(k, part)] = w_ref[pl.ds(r, high), cols] - factor * grad
        out_copy(i).start()

    for i in range(max(tiles - slots, 0), tiles):
        out_copy(i).wait()


def on_device(n_in, n_out, inputs, weight, out_grad, step_size):
    depth, width = weight.shape
    rows_x, rows = inputs.shape[0], out_grad.shape[0]
    total = rows * n_in
    line = n_in // 2
    scale = float(depth * n_in) ** -0.5
    strip = fit(width, 128, 1024)
    strips = width // strip
    first = fit(width, 128, width // 2)
    vmem = pl.BlockSpec(memory_space=pltpu.VMEM)
    hbm = pl.BlockSpec(memory_space=pl.ANY)
    shape = jax.ShapeDtypeStruct
    dma = pltpu.SemaphoreType.DMA
    outs = pl.pallas_call(
        functools.partial(read_side, n_in, n_out, scale, first),
        out_shape=(
            pltpu.VMEM((depth, width), F32),
            shape((8, 128), F32),
            shape((depth, total), BF16),
            shape((total, width), BF16),
            *[shape((rows, width), BF16)] * line,
            *[shape((rows_x, depth), BF16)] * n_out,
        ),
        in_specs=[pl.BlockSpec(memory_space=pltpu.SMEM), vmem, vmem, hbm],
        out_specs=(vmem,) * (4 + line + n_out),
        scratch_shapes=[
            pltpu.VMEM((n_out, rows_x, depth), BF16),
            pltpu.VMEM((total, depth), BF16),
            pltpu.VMEM((n_in, rows, width), BF16),
            pltpu.VMEM((line, 2, rows, strip), F32),
            pltpu.VMEM((strips, line * rows, strip), BF16),
            pltpu.VMEM((strips, line * rows, strip), BF16),
            pltpu.VMEM((strips, line, rows, strip), F32),
            pltpu.VMEM((n_out, rows_x, depth), F32),
            dma((strips,)), dma((n_out,)), dma((n_out,)),
            dma((n_in, 2, 3)), dma((n_in, 2)), dma((strips,)), dma((strips,)),
        ],
        compiler_params=pltpu.CompilerParams(
            collective_id=0, has_side_effects=True, vmem_limit_bytes=9_000_000),
        cost_estimate=pl.CostEstimate(
            flops=4 * total * depth * width, bytes_accessed=4 * depth * width, transcendentals=0),
    )(step_size.reshape(1), inputs, out_grad, weight)
    kept, factor, xt, grads = outs[:4]
    ysum, ipart = outs[4 : 4 + line], outs[4 + line :]
    kept = pltpu.with_memory_space_constraint(kept, pltpu.VMEM)

    def along(t):
        return [(2 * a + b, 2 * ((a + t) % line) + b) for a in range(line) for b in range(2)]

    terms = [ysum[0]] + [lax.ppermute(ysum[t], "in", along(t)) for t in range(1, line)]
    backs = [ipart[0]] + [
        lax.ppermute(ipart[t], "out", [(a, (a + t) % n_out) for a in range(n_out)])
        for t in range(1, n_out)]

    high, wide = fit(depth, 8, 256), fit(width, 128, 1024)
    new_weight = pl.pallas_call(
        write_side,
        out_shape=shape((depth, width), F32),
        in_specs=[vmem, vmem, vmem, vmem],
        out_specs=hbm,
        scratch_shapes=[pltpu.VMEM((4, high, wide), F32), dma((4,))],
        compiler_params=pltpu.CompilerParams(vmem_limit_bytes=8_000_000),
        cost_estimate=pl.CostEstimate(
            flops=2 * total * depth * width, bytes_accessed=4 * depth * width, transcendentals=0),
    )(factor, kept, xt, grads)

    projected = functools.reduce(jnp.add, [t.astype(F32) for t in terms]).astype(BF16)
    input_grad = functools.reduce(jnp.add, [t.astype(F32) for t in backs]).astype(BF16)
    return projected, input_grad, new_weight


def solution(mesh):
    placed = (P("out", "in"), P("in", "out"), P("in", "out"), P())
    return jax.shard_map(
        functools.partial(on_device, mesh.shape["in"], mesh.shape["out"]),
        mesh=mesh,
        in_specs=placed,
        out_specs=(P("in", "out"), P("out", "in"), P("in", "out")),
        check_vma=False,
    )
```

```python
import functools

import jax
import jax.numpy as jnp
from jax import lax
from jax.experimental import pallas as pl
from jax.experimental.pallas import tpu as pltpu
from jax.sharding import PartitionSpec as P

MESH = pl.DeviceIdType.MESH
BF16, F32 = jnp.bfloat16, jnp.float32
LEFT, RIGHT, ACROSS = 0, 1, 2


def fit(extent, unit, most):
    return max(c for c in range(unit, most + 1, unit) if extent % c == 0)


def read_side(
    n_in, n_out, scale, first,
    step_ref, x_ref, g_ref, w_ref,
    wv_ref, factor_ref, xt_ref, gall_ref, *rest,
):
    line = n_in // 2
    (proj_ref, ig_ref, x3, x64, g3, part, send, recv, kept, back, zsend, zrecv, isend, irecv,
     w_sem, xs_sem, xr_sem, gs_sem, gr_sem, ys_sem, yr_sem,
     zs_sem, zr_sem, is_sem, ir_sem) = rest
    depth, width = wv_ref.shape
    rows = g_ref.shape[0]
    rows_x = x_ref.shape[0]
    strips, _, strip = send.shape
    sub = fit(strip, 128, 512)
    me = lax.axis_index("in")
    mo = lax.axis_index("out")
    p, y = me // 2, me % 2
    pair = me + 1 - 2 * y

    def w_copy(s):
        cols = pl.ds(s * strip, strip)
        return pltpu.make_async_copy(w_ref.at[:, cols], wv_ref.at[:, cols], w_sem.at[s])

    ahead = min(3, strips)
    for s in range(ahead):
        w_copy(s).start()

    barrier = pltpu.get_barrier_semaphore()
    peers = [{"in": pair}] + [{"in": lax.rem(me + 2 * t, n_in)} for t in range(1, line)]
    peers += [{"out": lax.rem(mo + t, n_out)} for t in range(1, n_out)]
    for peer in peers:
        pl.semaphore_signal(barrier, inc=1, device_id=peer, device_id_type=MESH)
    pl.semaphore_wait(barrier, len(peers))

    def x_copy(t):
        return pltpu.make_async_remote_copy(
            src_ref=x_ref, dst_ref=x3.at[mo], send_sem=xs_sem.at[t], recv_sem=xr_sem.at[mo],
            device_id={"out": lax.rem(mo + t, n_out)}, device_id_type=MESH)

    def x_arrival(t):
        o = lax.rem(mo + n_out - t, n_out)
        return pltpu.make_async_remote_copy(
            src_ref=x_ref, dst_ref=x3.at[o], send_sem=xs_sem.at[t], recv_sem=xr_sem.at[o],
            device_id={"out": o}, device_id_type=MESH)

    for t in range(1, n_out):
        x_copy(t).start()

    groups = [pl.ds(0, first), pl.ds(first, width - first)]

    def g_copy(i, group, way, own=False):
        cols = groups[group]
        target = {LEFT: lax.rem(me + n_in - 2, n_in), RIGHT: lax.rem(me + 2, n_in), ACROSS: pair}[way]
        here = g3.at[i, :, cols]
        return pltpu.make_async_remote_copy(
            src_ref=g_ref.at[:, cols] if own else here, dst_ref=here,
            send_sem=gs_sem.at[i, group, way], recv_sem=gr_sem.at[i, group],
            device_id={"in": target}, device_id_type=MESH)

    def outward(i, group, way, verb, own=False):
        edge = (p < line - 1) if way == RIGHT else (p > 0)

        @pl.when(edge)
        def _():
            getattr(g_copy(i, group, way, own), verb)()

    def origin_step(verb):
        for group in (1, 0):
            getattr(g_copy(me, group, ACROSS, True), verb)()
        for group in (1, 0):
            outward(me, group, LEFT, verb, True)
            outward(me, group, RIGHT, verb, True)

    def pair_step(verb):
        if verb == "start":
            g_copy(pair, 1, ACROSS).wait_recv()
        outward(pair, 1, LEFT, verb)
        outward(pair, 1, RIGHT, verb)

    def hop_step(s, verb):
        for way in (RIGHT, LEFT):
            o = p - s if way == RIGHT else p + s

            @pl.when((o >= 0) & (o < line))
            def _():
                for par in (y, 1 - y):
                    i = o * 2 + par
                    if verb == "start":
                        g_copy(i, 1, way).wait_recv()
                    outward(i, 1, way, verb)
                i = o * 2 + y
                if verb == "start":
                    g_copy(i, 0, way).wait_recv()
                outward(i, 0, way, verb)
                getattr(g_copy(i, 0, ACROSS), verb)()

    origin_step("start")
    factor_ref[...] = jnp.full(factor_ref.shape, step_ref[0] * scale, F32)
    x3[mo] = x_ref[...]
    g3[me] = g_ref[...]

    for t in range(1, n_out):
        x_arrival(t).wait_recv()
    rows_all = jnp.concatenate([x3[o].astype(F32) for o in range(n_out)], axis=0)
    x64[...] = rows_all.astype(BF16)
    xt_ref[...] = jnp.transpose(rows_all).astype(BF16)

    def y_copy(s):
        return pltpu.make_async_remote_copy(
            src_ref=send.at[s], dst_ref=recv.at[s], send_sem=ys_sem.at[s], recv_sem=yr_sem.at[s],
            device_id={"in": pair}, device_id_type=MESH)

    def forward(s):
        if s + ahead < strips:
            w_copy(s + ahead).start()
        w_copy(s).wait()

        @pl.loop(0, strip // sub)
        def _(b):
            c = pl.multiple_of(b * sub, sub)
            low = wv_ref[:, pl.ds(s * strip + c, sub)].astype(BF16)
            out = jnp.dot(x64[...], low, preferred_element_type=F32) * scale
            part[:, :, :, pl.ds(c, sub)] = out.reshape(line, 2, rows, sub)

        send[s] = part[:, 1 - y].reshape(line * rows, strip).astype(BF16)
        y_copy(s).start()
        kept[s] = part[:, y]

    def z_copy(s, t):
        return pltpu.make_async_remote_copy(
            src_ref=zsend.at[t - 1, s], dst_ref=zrecv.at[t - 1, s],
            send_sem=zs_sem.at[t - 1, s], recv_sem=zr_sem.at[t - 1, s],
            device_id={"in": lax.rem(me + 2 * t, n_in)}, device_id_type=MESH)

    def settle(s):
        y_copy(s).wait_recv()
        kept[s] = kept[s] + recv[s].astype(F32).reshape(line, rows, strip)
        for t in range(1, line):
            zsend[t - 1, s] = kept[s, lax.rem(p + t, line)].astype(BF16)
            z_copy(s, t).start()

    def i_copy(t):
        return pltpu.make_async_remote_copy(
            src_ref=isend.at[t - 1], dst_ref=irecv.at[t - 1],
            send_sem=is_sem.at[t - 1], recv_sem=ir_sem.at[t - 1],
            device_id={"out": lax.rem(mo + t, n_out)}, device_id_type=MESH)

    def backward(low_col, high_col):
        chunk = fit(high_col - low_col, 128, 512)

        @pl.loop(0, (high_col - low_col) // chunk)
        def _(b):
            cols = pl.ds(pl.multiple_of(low_col + b * chunk, 128), chunk)
            grads = jnp.concatenate(
                [g3[i, :, cols].astype(F32) for i in range(n_in)], axis=0).astype(BF16)
            gall_ref[:, cols] = grads
            low = wv_ref[:, cols].astype(BF16)
            out = lax.dot_general(grads, low, (((1,), (1,)), ((), ())),
                                  preferred_element_type=F32)
            back[...] += out.reshape(n_out, rows_x, depth)

    lag = 2
    back[...] = jnp.zeros_like(back)
    pair_step("start")
    hop = 1
    for s in range(strips):
        forward(s)
        while hop < line and hop * strips // line - 1 <= s:
            hop_step(hop, "start")
            hop += 1
        if s >= lag:
            settle(s - lag)

    backward(first, width)
    for s in range(max(strips - lag, 0), strips):
        settle(s)

    @pl.loop(0, line)
    def _(o):
        g_copy(o * 2 + 1 - y, 0, ACROSS).wait_recv()

    backward(0, first)
    for t in range(1, n_out):
        isend[t - 1] = (back[lax.rem(mo + t, n_out)] * scale).astype(BF16)
        i_copy(t).start()

    for s in range(strips):
        total = kept[s, p]
        for t in range(1, line):
            z_copy(s, t).wait_recv()
            total = total + zrecv[t - 1, s].astype(F32)
        proj_ref[:, pl.ds(s * strip, strip)] = total.astype(BF16)

    total = back[mo] * scale
    for t in range(1, n_out):
        i_copy(t).wait_recv()
        total = total + irecv[t - 1].astype(F32)
    ig_ref[...] = total.astype(BF16)

    for t in range(1, n_out):
        i_copy(t).wait_send()
    for t in range(1, n_out):
        x_copy(t).wait_send()
    origin_step("wait_send")
    pair_step("wait_send")
    for s in range(1, line):
        hop_step(s, "wait_send")
    for s in range(strips):
        y_copy(s).wait_send()
        for t in range(1, line):
            z_copy(s, t).wait_send()


def write_side(
    factor_ref, w_ref, xt_ref, g_ref, proj_ref, ig_ref,
    o_ref, proj_out, ig_out, stage, sem, small_sem,
):
    slots, high, wide = stage.shape
    depth, width = w_ref.shape
    across = width // wide
    part = fit(wide, 128, 256)
    tiles = (depth // high) * across
    factor = factor_ref[0:1, 0:1]
    small = [pltpu.make_async_copy(proj_ref, proj_out, small_sem.at[0]),
             pltpu.make_async_copy(ig_ref, ig_out, small_sem.at[1])]
    for copy in small:
        copy.start()

    def out_copy(i):
        r = pl.multiple_of((i // across) * high, high)
        c = pl.multiple_of((i % across) * wide, wide)
        return pltpu.make_async_copy(
            stage.at[i % slots], o_ref.at[pl.ds(r, high), pl.ds(c, wide)], sem.at[i % slots])

    @pl.loop(0, tiles)
    def _(i):
        @pl.when(i >= slots)
        def _():
            out_copy(i - slots).wait()

        r = pl.multiple_of((i // across) * high, high)
        c = pl.multiple_of((i % across) * wide, wide)
        left = xt_ref[pl.ds(r, high), :]
        for k in range(0, wide, part):
            cols = pl.ds(c + k, part)
            grad = jnp.dot(left, g_ref[:, cols], preferred_element_type=F32)
            stage[i % slots, :, pl.ds(k, part)] = w_ref[pl.ds(r, high), cols] - factor * grad
        out_copy(i).start()

    for i in range(max(tiles - slots, 0), tiles):
        out_copy(i).wait()
    for copy in small:
        copy.wait()


def on_device(n_in, n_out, inputs, weight, out_grad, step_size):
    depth, width = weight.shape
    rows_x, rows = inputs.shape[0], out_grad.shape[0]
    total = rows * n_in
    line = n_in // 2
    scale = float(depth * n_in) ** -0.5
    strip = fit(width, 128, 1024)
    strips = width // strip
    first = fit(width, 128, width // 2)
    room = min(40_000_000, 64_223_104 - 4 * depth * width)
    vmem = pl.BlockSpec(memory_space=pltpu.VMEM)
    hbm = pl.BlockSpec(memory_space=pl.ANY)
    shape = jax.ShapeDtypeStruct
    dma = pltpu.SemaphoreType.DMA
    outs = pl.pallas_call(
        functools.partial(read_side, n_in, n_out, scale, first),
        out_shape=(
            pltpu.VMEM((depth, width), F32),
            pltpu.VMEM((8, 128), F32),
            pltpu.VMEM((depth, total), BF16),
            pltpu.VMEM((total, width), BF16),
            pltpu.VMEM((rows, width), BF16),
            pltpu.VMEM((rows_x, depth), BF16),
        ),
        in_specs=[pl.BlockSpec(memory_space=pltpu.SMEM), vmem, vmem, hbm],
        out_specs=(vmem,) * 6,
        scratch_shapes=[
            pltpu.VMEM((n_out, rows_x, depth), BF16),
            pltpu.VMEM((total, depth), BF16),
            pltpu.VMEM((n_in, rows, width), BF16),
            pltpu.VMEM((line, 2, rows, strip), F32),
            pltpu.VMEM((strips, line * rows, strip), BF16),
            pltpu.VMEM((strips, line * rows, strip), BF16),
            pltpu.VMEM((strips, line, rows, strip), F32),
            pltpu.VMEM((n_out, rows_x, depth), F32),
            pltpu.VMEM((line - 1, strips, rows, strip), BF16),
            pltpu.VMEM((line - 1, strips, rows, strip), BF16),
            pltpu.VMEM((n_out - 1, rows_x, depth), BF16),
            pltpu.VMEM((n_out - 1, rows_x, depth), BF16),
            dma((strips,)), dma((n_out,)), dma((n_out,)),
            dma((n_in, 2, 3)), dma((n_in, 2)), dma((strips,)), dma((strips,)),
            dma((line - 1, strips)), dma((line - 1, strips)), dma((n_out - 1,)), dma((n_out - 1,)),
        ],
        compiler_params=pltpu.CompilerParams(
            collective_id=0, has_side_effects=True, vmem_limit_bytes=room),
        cost_estimate=pl.CostEstimate(
            flops=4 * total * depth * width, bytes_accessed=4 * depth * width, transcendentals=0),
    )(step_size.reshape(1), inputs, out_grad, weight)
    kept, factor, xt, grads, proj, back = [
        pltpu.with_memory_space_constraint(o, pltpu.VMEM) for o in outs]

    high, wide = fit(depth, 8, 256), fit(width, 128, 1024)
    new_weight, projected, input_grad = pl.pallas_call(
        write_side,
        out_shape=(
            shape((depth, width), F32), shape((rows, width), BF16), shape((rows_x, depth), BF16)),
        in_specs=[vmem] * 6,
        out_specs=(hbm,) * 3,
        scratch_shapes=[pltpu.VMEM((4, high, wide), F32), dma((4,)), dma((2,))],
        compiler_params=pltpu.CompilerParams(vmem_limit_bytes=room),
        cost_estimate=pl.CostEstimate(
            flops=2 * total * depth * width, bytes_accessed=4 * depth * width, transcendentals=0),
    )(factor, kept, xt, grads, proj, back)

    return projected, input_grad, new_weight


def solution(mesh):
    placed = (P("out", "in"), P("in", "out"), P("in", "out"), P())
    return jax.shard_map(
        functools.partial(on_device, mesh.shape["in"], mesh.shape["out"]),
        mesh=mesh,
        in_specs=placed,
        out_specs=(P("in", "out"), P("out", "in"), P("in", "out")),
        check_vma=False,
    )
```
